32 devices in a mesh: group: 2 (over y), ctx: 4 (over z), head: 4 (over x, core).
Axes of the slice: x: 2, y: 2, z: 4, core: 2. Of those that a mesh axis runs over, the one named last changes fastest.
Arguments:
- queries: bfloat16 [4096, 8192], P(('group', 'ctx'), 'head'), parts along dimension 0, may hold values from -6 to 6
- key_vectors: bfloat16 [4096, 8192], P(('group', 'ctx'), 'head'), parts along dimension 0, may hold values from -0.5 to 0.5
- value_vectors: bfloat16 [4096, 8192], P(('group', 'ctx'), 'head'), parts along dimension 0, may hold values from -6 to 6
- log_decay: float32 [4096, 64], P(('group', 'ctx'), 'head'), parts along dimension 0, may hold values from -1.5 to 0, as said below
- out_gain: float32 [8192], P('head'), may hold values from 0.5 to 1.5
Outputs:
- folded_out: bfloat16 [4096, 8192], P(('group', 'ctx'), 'head'), parts along dimension 0
The draws below stay inside these ranges and needn't reach their ends.
There are 2 independent parts, one for each index of `group`. The reference program is written for one: setup_inputs(seed, part) draws one part's arguments, and reference() takes and returns one part's arrays. A program takes and returns all parts, laid end to end along the dimension named above; an argument that names none is the same for every part. Nothing has to cross between parts.
Inputs may be any that keep to these rules, and one draw needn't show every extreme that they name: `log_decay`: log decay of each head's state at each token; never positive.
All inputs are finite; a program needn't handle non-finite values.
Results may differ from the reference program's by a relative error of at most 0.0056.
Values may be sent and summed in bfloat16 or wider, within the bound.
A program may use at most 64 MiB of HBM per device.

```python
import jax
import jax.numpy as jnp
from jax import lax

HEAD_TOTAL = 64
DH = 128
TOK_DEV = 512
BLOCK = 512
SEQUENCE_TOKENS = 2048
N_CTX = 4


def draw_log_decay(key, part):
    random_child_keys = jax.random.split(key, 8)
    fast_share = 0.25
    middle_share = 0.25
    picker = jax.random.uniform(random_child_keys[0], (HEAD_TOTAL,))
    fast_rate = jnp.exp(jax.random.uniform(random_child_keys[1], (HEAD_TOTAL,), minval=jnp.log(1.0 / 50.0), maxval=jnp.log(1.0 / 30.0)))
    middle_rate = jnp.exp(jax.random.uniform(random_child_keys[6], (HEAD_TOTAL,), minval=jnp.log(1.0 / 4096.0), maxval=jnp.log(1.0 / 256.0)))
    slow_rate = 1.0 / SEQUENCE_TOKENS * jnp.exp(jax.random.uniform(random_child_keys[2], (HEAD_TOTAL,), minval=jnp.log(0.5), maxval=jnp.log(1.0)))
    baseline_decay_rate = jnp.where(picker < fast_share, fast_rate, jnp.where(picker < fast_share + middle_share, middle_rate, slow_rate))
    block_scale_factor = jax.random.uniform(random_child_keys[7], (SEQUENCE_TOKENS // TOK_DEV, HEAD_TOTAL), minval=0.5, maxval=1.5)
    block_scale_factor = jnp.repeat(block_scale_factor, TOK_DEV, axis=0)
    random_perturbation = jax.random.uniform(random_child_keys[3], (SEQUENCE_TOKENS, HEAD_TOTAL), minval=0.5, maxval=1.5)
    spike_positions = jax.random.randint(random_child_keys[4], (2, HEAD_TOTAL), 0, SEQUENCE_TOKENS)
    spike_decay_drop = jnp.log(jax.random.uniform(random_child_keys[5], (2, HEAD_TOTAL), minval=0.55, maxval=0.8))
    token_positions = jnp.arange(SEQUENCE_TOKENS)[:, None, None] == spike_positions[None]
    decay_spikes = jnp.sum(jnp.where(token_positions, spike_decay_drop[None], 0.0), axis=1)
    return (decay_spikes - baseline_decay_rate[None, :] * block_scale_factor * random_perturbation).astype(jnp.float32)


def level_of(key, dims, pieces, smallest, top_value):
    level, own = 1.0, jax.random.fold_in(key, 6)
    for axis_at, shards_of in pieces:
        steps = jnp.exp(jax.random.uniform(jax.random.fold_in(own, axis_at), (shards_of,), jnp.float32, smallest / len(pieces), top_value / len(pieces)))
        level = level * jnp.repeat(steps, dims[axis_at] // shards_of).reshape([-1 if axis == axis_at else 1 for axis in range(len(dims))])
    return level


def centred(rng, shape, scale, limit, cuts=(), kind=jnp.bfloat16):
    entries = scale * jax.random.normal(rng, shape, jnp.float32)
    if cuts:
        entries = entries * level_of(rng, shape, cuts, -0.22, 0.18)
    return jnp.clip(entries, -limit, limit).astype(kind)


def setup_inputs(seed: int = 0, part: int = 0) -> dict:
    streams_of = jax.random.split(jax.random.key(seed), 6)
    own_keys = jax.random.split(jax.random.fold_in(streams_of[5], part), 6)
    queries = centred(own_keys[0], (SEQUENCE_TOKENS, HEAD_TOTAL * DH), 1.0, 6.0, ((0, 4), (1, 4)))
    key_vectors = centred(own_keys[1], (SEQUENCE_TOKENS, HEAD_TOTAL * DH), DH ** -0.5, 0.5, ((0, 4), (1, 4)))
    value_vectors = centred(own_keys[2], (SEQUENCE_TOKENS, HEAD_TOTAL * DH), 1.0, 6.0, ((0, 4), (1, 4)))
    log_decay = draw_log_decay(jax.random.fold_in(jax.random.fold_in(streams_of[5], part), 71), part)
    out_gain = jnp.clip(1.0 + 0.1 * jax.random.normal(streams_of[4], (HEAD_TOTAL * DH,), jnp.float32), 0.5, 1.5)
    return {"queries": queries, "key_vectors": key_vectors, "value_vectors": value_vectors, "log_decay": log_decay, "out_gain": out_gain}


def block_step(carried, block):
    query_rows, key_rows, value_rows, decay_rows = block
    cum_decay = jnp.cumsum(decay_rows, axis=0)
    block_total = cum_decay[-1]
    scores = jnp.einsum('thd,shd->hts', query_rows.astype(jnp.float32), key_rows.astype(jnp.float32))
    decay_heads = jnp.transpose(cum_decay)
    differ = decay_heads[:, :, None] - decay_heads[:, None, :]
    causal = jnp.arange(BLOCK)[:, None] >= jnp.arange(BLOCK)[None, :]
    weights = jnp.where(causal[None], jnp.exp(jnp.minimum(differ, 0.0)), 0.0)
    probs = (scores * weights).astype(jnp.bfloat16)
    intra = jnp.einsum('hts,shd->thd', probs.astype(jnp.float32), value_rows.astype(jnp.float32))
    key_decayed = (key_rows.astype(jnp.float32) * jnp.exp(block_total[None, :] - cum_decay)[:, :, None]).astype(jnp.bfloat16)
    local_state = jnp.einsum('shd,she->hde', key_decayed.astype(jnp.float32), value_rows.astype(jnp.float32))
    query_decayed = (query_rows.astype(jnp.float32) * jnp.exp(cum_decay)[:, :, None]).astype(jnp.bfloat16)
    carried_low = carried.astype(jnp.bfloat16)
    inter = jnp.einsum('thd,hde->the', query_decayed.astype(jnp.float32), carried_low.astype(jnp.float32))
    attn = intra + inter
    following = jnp.exp(block_total)[:, None, None] * carried + local_state
    return (following, attn)

def reference(queries, key_vectors, value_vectors, log_decay, out_gain):
    block_count = SEQUENCE_TOKENS // BLOCK
    shaped = (block_count, BLOCK, HEAD_TOTAL, DH)
    blocks = (queries.reshape(shaped), key_vectors.reshape(shaped), value_vectors.reshape(shaped), log_decay.reshape(block_count, BLOCK, HEAD_TOTAL))
    start = jnp.zeros((HEAD_TOTAL, DH, DH), jnp.float32)
    finish, attn = lax.scan(block_step, start, blocks)
    attn = attn.reshape(SEQUENCE_TOKENS, HEAD_TOTAL, DH)
    mean_square = lax.optimization_barrier(jnp.mean(attn * attn, axis=-1, keepdims=True))
    normed = attn * lax.rsqrt(mean_square + 1e-06) * out_gain.reshape(HEAD_TOTAL, DH)[None]
    normed = normed.reshape(SEQUENCE_TOKENS, HEAD_TOTAL * DH).astype(jnp.bfloat16)
    half_count = 2 * N_CTX
    halves = normed.reshape(half_count, SEQUENCE_TOKENS // half_count, HEAD_TOTAL * DH)
    token_positions = jnp.arange(half_count).astype(jnp.int32)
    source = jnp.where(token_positions % 2 == 0, token_positions, half_count - token_positions).astype(jnp.int32)
    return jnp.take(halves, source, axis=0).reshape(SEQUENCE_TOKENS, HEAD_TOTAL * DH)
```

```python
import functools

import jax
import jax.numpy as jnp
from jax import lax
from jax.experimental import pallas as pl
from jax.experimental.pallas import tpu as pltpu
from jax.sharding import PartitionSpec as P

BLOCK = 512
MESH = pl.DeviceIdType.MESH
F32 = jnp.float32
BF16 = jnp.bfloat16
CONTRACT_LAST = (((1,), (1,)), ((), ()))
CONTRACT_FIRST = (((0,), (0,)), ((), ()))


def kernel(
    count, heads, pack, wire,
    q_hbm, k_hbm, v_hbm, decay_ref, gain_ref, out_hbm,
    q, k, v, colb, rowc, local, rbuf, sbuf, first, second, ibuf,
    load_sem, state_send, state_recv, out_send, out_recv, first_sem,
):
    rows, features = q.shape
    width = features // heads
    half = rows // 2
    steps = heads // pack
    span = pack * width
    me = lax.axis_index("ctx")
    mirror = count - 1 - me
    is_first = me == 0
    is_last = me == count - 1

    def cols(step):
        return pl.ds(pl.multiple_of(step * span, span), span)

    def head_cols(head):
        return pl.ds(pl.multiple_of(head * width, width), width)

    def load(which, step):
        src, dst = ((k_hbm, k), (v_hbm, v), (q_hbm, q))[which]
        return pltpu.make_async_copy(
            src.at[:, cols(step)], dst.at[:, cols(step)], load_sem.at[which, step]
        )

    def state_copy(step):
        return pltpu.make_async_remote_copy(
            src_ref=sbuf.at[step],
            dst_ref=rbuf.at[step],
            send_sem=state_send.at[step],
            recv_sem=state_recv.at[step],
            device_id={"ctx": me + 1},
            device_id_type=MESH,
        )

    def out_copy(step):
        return pltpu.make_async_remote_copy(
            src_ref=second.at[:, cols(step)],
            dst_ref=out_hbm.at[pl.ds(half, half), cols(step)],
            send_sem=out_send.at[step],
            recv_sem=out_recv.at[step],
            device_id={"ctx": mirror},
            device_id_type=MESH,
        )

    def first_copy(step):
        return pltpu.make_async_copy(
            first.at[:, cols(step)], out_hbm.at[pl.ds(0, half), cols(step)], first_sem.at[step]
        )

    barrier = pltpu.get_barrier_semaphore()

    @pl.when(jnp.logical_not(is_first))
    def _():
        pl.semaphore_signal(barrier, inc=1, device_id={"ctx": me - 1}, device_id_type=MESH)

    @pl.when(jnp.logical_not(is_last))
    def _():
        pl.semaphore_signal(barrier, inc=1, device_id={"ctx": me + 1}, device_id_type=MESH)

    pl.semaphore_signal(barrier, inc=1, device_id={"ctx": mirror}, device_id_type=MESH)

    @pl.loop(0, steps)
    def _(step):
        load(0, step).start()
        load(1, step).start()

    @pl.loop(0, steps)
    def _(step):
        load(2, step).start()

    earlier = lax.broadcasted_iota(jnp.int32, (rows, rows), 0)
    later = lax.broadcasted_iota(jnp.int32, (rows, rows), 1)
    upto = jnp.where(earlier <= later, 1.0, 0.0).astype(BF16)
    rest = decay_ref[...]
    cum = jnp.zeros((heads, rows), F32)
    for _ in range(3):
        piece = rest.astype(BF16)
        rest = rest - piece.astype(F32)
        cum = cum + jnp.dot(piece, upto, preferred_element_type=F32)
    rowc[...] = jnp.zeros_like(rowc)
    rowc[0:heads, :] = cum
    columns = rowc[...].T
    for head in range(heads):
        colb[head] = jnp.broadcast_to(columns[:, head : head + 1], (rows, width))

    @pl.when(is_first)
    def _():
        rbuf[...] = jnp.zeros_like(rbuf)

    peers = 1 + (me + count - 1) // count + (mirror + count - 1) // count
    pl.semaphore_wait(barrier, peers)

    @pl.loop(0, steps)
    def _(step):
        load(0, step).wait()
        load(1, step).wait()
        for j in range(pack):
            head = step * pack + j
            here = head_cols(head)
            total = colb[head, rows - 1 : rows, :]
            decayed = (k[:, here].astype(F32) * jnp.exp(total - colb[head])).astype(BF16)
            state = lax.dot_general(decayed, v[:, here], CONTRACT_FIRST, preferred_element_type=F32)
            local[head] = state

            @pl.when(is_first)
            def _():
                sbuf[step, j] = state.astype(wire)

        @pl.when(is_first)
        def _():
            state_copy(step).start()

    causal = lax.broadcasted_iota(jnp.int32, (half, half), 0) >= lax.broadcasted_iota(
        jnp.int32, (half, half), 1
    )

    def probs(head, low, start):
        queries = q[low : low + half, head_cols(head)]
        keys = k[start : start + half, head_cols(head)]
        scores = lax.dot_general(queries, keys, CONTRACT_LAST, preferred_element_type=F32)
        mine = colb[head, low : low + half, :]
        mine = jnp.concatenate([mine] * (half // width), axis=1)
        theirs = rowc[pl.ds(head, 1), start : start + half]
        weights = jnp.exp(jnp.minimum(mine - theirs, 0.0))
        if low == start:
            weights = jnp.where(causal, weights, 0.0)
        return (scores * weights).astype(BF16)

    def intra(head, low, start):
        return jnp.dot(
            probs(head, low, start),
            v[start : start + half, head_cols(head)],
            preferred_element_type=F32,
        )

    def finish(head, low, within, carried):
        queries = q[low : low + half, head_cols(head)].astype(F32)
        decayed = (queries * jnp.exp(colb[head, low : low + half, :])).astype(BF16)
        attn = within + jnp.dot(decayed, carried, preferred_element_type=F32)
        mean_square = jnp.mean(attn * attn, axis=-1, keepdims=True)
        normed = attn * lax.rsqrt(mean_square + 1e-06) * gain_ref[pl.ds(head, 1), :]
        return normed.astype(BF16)

    @pl.loop(0, steps)
    def _(step):
        load(2, step).wait()
        for j in range(pack):
            head = step * pack + j
            ibuf[j] = intra(head, half, 0) + intra(head, half, half)

        @pl.when(jnp.logical_not(is_first))
        def _():
            state_copy(step).wait_recv()

            @pl.when(jnp.logical_not(is_last))
            def _():
                for j in range(pack):
                    head = step * pack + j
                    total = jnp.exp(colb[head, rows - 1 : rows, :])
                    following = total * rbuf[step, j].astype(F32) + local[head]
                    sbuf[step, j] = following.astype(wire)
                state_copy(step).start()

        for j in range(pack):
            head = step * pack + j
            second[:, head_cols(head)] = finish(head, half, ibuf[j], rbuf[step, j].astype(BF16))
        out_copy(step).start()

    @pl.loop(0, steps)
    def _(step):
        for j in range(pack):
            head = step * pack + j
            within = intra(head, 0, 0)
            first[:, head_cols(head)] = finish(head, 0, within, rbuf[step, j].astype(BF16))
        first_copy(step).start()

    @pl.loop(0, steps)
    def _(step):
        first_copy(step).wait()
        out_copy(step).wait_send()

        @pl.when(jnp.logical_not(is_last))
        def _():
            state_copy(step).wait_send()

    @pl.loop(0, steps)
    def _(step):
        out_copy(step).wait_recv()


def shards(count, queries, key_vectors, value_vectors, log_decay, out_gain):
    rows, features = queries.shape
    heads = log_decay.shape[1]
    width = features // heads
    pack = 2
    steps = heads // pack
    half = rows // 2
    wire = BF16 if count <= 8 else F32
    assert rows == BLOCK and count % 2 == 0 and heads % pack == 0
    anywhere = pl.BlockSpec(memory_space=pl.ANY)
    vmem = pl.BlockSpec(memory_space=pltpu.VMEM)
    return pl.pallas_call(
        functools.partial(kernel, count, heads, pack, wire),
        out_shape=jax.ShapeDtypeStruct((rows, features), BF16),
        in_specs=[anywhere, anywhere, anywhere, vmem, vmem],
        out_specs=anywhere,
        scratch_shapes=[
            pltpu.VMEM((rows, features), BF16),
            pltpu.VMEM((rows, features), BF16),
            pltpu.VMEM((rows, features), BF16),
            pltpu.VMEM((heads, rows, width), F32),
            pltpu.VMEM((128, rows), F32),
            pltpu.VMEM((heads, width, width), F32),
            pltpu.VMEM((steps, pack, width, width), wire),
            pltpu.VMEM((steps, pack, width, width), wire),
            pltpu.VMEM((half, features), BF16),
            pltpu.VMEM((half, features), BF16),
            pltpu.VMEM((pack, half, width), F32),
            pltpu.SemaphoreType.DMA((3, steps)),
            pltpu.SemaphoreType.DMA((steps,)),
            pltpu.SemaphoreType.DMA((steps,)),
            pltpu.SemaphoreType.DMA((steps,)),
            pltpu.SemaphoreType.DMA((steps,)),
            pltpu.SemaphoreType.DMA((steps,)),
        ],
        compiler_params=pltpu.CompilerParams(
            collective_id=0, has_side_effects=True, vmem_limit_bytes=40 << 20
        ),
    )(queries, key_vectors, value_vectors, log_decay.T, out_gain.reshape(heads, width))


def solution(mesh):
    in_specs = (
        P(("group", "ctx"), "head"),
        P(("group", "ctx"), "head"),
        P(("group", "ctx"), "head"),
        P(("group", "ctx"), "head"),
        P("head"),
    )
    out_specs = P(("group", "ctx"), "head")
    return jax.shard_map(
        functools.partial(shards, mesh.shape["ctx"]),
        mesh=mesh,
        in_specs=in_specs,
        out_specs=out_specs,
        check_vma=False,
    )
```

```python
import functools

import jax
import jax.numpy as jnp
from jax import lax
from jax.experimental import pallas as pl
from jax.experimental.pallas import tpu as pltpu
from jax.sharding import PartitionSpec as P

BLOCK = 512
MESH = pl.DeviceIdType.MESH
F32 = jnp.float32
BF16 = jnp.bfloat16
CONTRACT_LAST = (((1,), (1,)), ((), ()))
CONTRACT_FIRST = (((0,), (0,)), ((), ()))


def kernel(
    count, heads, pack, wire,
    q_hbm, k_hbm, v_hbm, decay_ref, gain_ref, out_hbm,
    q, k, v, colb, rowc, local, rbuf, sbuf, first, second, ibuf,
    load_sem, state_send, state_recv, out_send, out_recv, first_sem,
):
    rows, features = q.shape
    width = features // heads
    half = rows // 2
    steps = heads // pack
    span = pack * width
    me = lax.axis_index("ctx")
    mirror = count - 1 - me
    is_first = me == 0
    is_last = me == count - 1
    holds = jnp.logical_and(me > 0, me < mirror)

    def cols(step):
        return pl.ds(pl.multiple_of(step * span, span), span)

    def head_cols(head):
        return pl.ds(pl.multiple_of(head * width, width), width)

    def load(which, step):
        src, dst = ((k_hbm, k), (v_hbm, v), (q_hbm, q))[which]
        return pltpu.make_async_copy(
            src.at[:, cols(step)], dst.at[:, cols(step)], load_sem.at[which, step]
        )

    def state_copy(step):
        return pltpu.make_async_remote_copy(
            src_ref=sbuf.at[step],
            dst_ref=rbuf.at[step],
            send_sem=state_send.at[step],
            recv_sem=state_recv.at[step],
            device_id={"ctx": me + 1},
            device_id_type=MESH,
        )

    def out_copy(step):
        return pltpu.make_async_remote_copy(
            src_ref=second.at[:, cols(step)],
            dst_ref=out_hbm.at[pl.ds(half, half), cols(step)],
            send_sem=out_send.at[step],
            recv_sem=out_recv.at[step],
            device_id={"ctx": mirror},
            device_id_type=MESH,
        )

    def first_copy(step):
        return pltpu.make_async_copy(
            first.at[:, cols(step)], out_hbm.at[pl.ds(0, half), cols(step)], first_sem.at[step]
        )

    barrier = pltpu.get_barrier_semaphore()

    @pl.when(jnp.logical_not(is_first))
    def _():
        pl.semaphore_signal(barrier, inc=1, device_id={"ctx": me - 1}, device_id_type=MESH)

    @pl.when(jnp.logical_not(is_last))
    def _():
        pl.semaphore_signal(barrier, inc=1, device_id={"ctx": me + 1}, device_id_type=MESH)

    pl.semaphore_signal(barrier, inc=1, device_id={"ctx": mirror}, device_id_type=MESH)

    @pl.loop(0, steps)
    def _(step):
        load(0, step).start()
        load(1, step).start()

    @pl.loop(0, steps)
    def _(step):
        load(2, step).start()

    earlier = lax.broadcasted_iota(jnp.int32, (rows, rows), 0)
    later = lax.broadcasted_iota(jnp.int32, (rows, rows), 1)
    upto = jnp.where(earlier <= later, 1.0, 0.0).astype(BF16)
    rest = decay_ref[...]
    cum = jnp.zeros((heads, rows), F32)
    for _ in range(3):
        piece = rest.astype(BF16)
        rest = rest - piece.astype(F32)
        cum = cum + jnp.dot(piece, upto, preferred_element_type=F32)
    rowc[...] = jnp.zeros_like(rowc)
    rowc[0:heads, :] = cum
    columns = rowc[...].T
    for head in range(heads):
        colb[head] = jnp.broadcast_to(columns[:, head : head + 1], (rows, width))

    @pl.when(is_first)
    def _():
        rbuf[...] = jnp.zeros_like(rbuf)

    peers = 1 + (me + count - 1) // count + (mirror + count - 1) // count
    pl.semaphore_wait(barrier, peers)

    @pl.loop(0, steps)
    def _(step):
        load(0, step).wait()
        load(1, step).wait()
        for j in range(pack):
            head = step * pack + j
            here = head_cols(head)
            total = colb[head, rows - 1 : rows, :]
            decayed = (k[:, here].astype(F32) * jnp.exp(total - colb[head])).astype(BF16)
            state = lax.dot_general(decayed, v[:, here], CONTRACT_FIRST, preferred_element_type=F32)
            local[head] = state

            @pl.when(is_first)
            def _():
                sbuf[step, j] = state.astype(wire)

        @pl.when(is_first)
        def _():
            state_copy(step).start()

    causal = lax.broadcasted_iota(jnp.int32, (half, half), 0) >= lax.broadcasted_iota(
        jnp.int32, (half, half), 1
    )

    def probs(head, low, start):
        queries = q[low : low + half, head_cols(head)]
        keys = k[start : start + half, head_cols(head)]
        scores = lax.dot_general(queries, keys, CONTRACT_LAST, preferred_element_type=F32)
        mine = colb[head, low : low + half, :]
        mine = jnp.concatenate([mine] * (half // width), axis=1)
        theirs = rowc[pl.ds(head, 1), start : start + half]
        weights = jnp.exp(jnp.minimum(mine - theirs, 0.0))
        if low == start:
            weights = jnp.where(causal, weights, 0.0)
        return (scores * weights).astype(BF16)

    def intra(head, low, start):
        return jnp.dot(
            probs(head, low, start),
            v[start : start + half, head_cols(head)],
            preferred_element_type=F32,
        )

    def finish(head, low, within, carried):
        queries = q[low : low + half, head_cols(head)].astype(F32)
        decayed = (queries * jnp.exp(colb[head, low : low + half, :])).astype(BF16)
        attn = within + jnp.dot(decayed, carried, preferred_element_type=F32)
        mean_square = jnp.mean(attn * attn, axis=-1, keepdims=True)
        normed = attn * lax.rsqrt(mean_square + 1e-06) * gain_ref[pl.ds(head, 1), :]
        return normed.astype(BF16)

    @pl.loop(0, steps)
    def _(step):
        load(2, step).wait()
        for j in range(pack):
            head = step * pack + j
            ibuf[j] = intra(head, half, 0) + intra(head, half, half)

        @pl.when(jnp.logical_not(is_first))
        def _():
            state_copy(step).wait_recv()

            @pl.when(jnp.logical_not(is_last))
            def _():
                for j in range(pack):
                    head = step * pack + j
                    total = jnp.exp(colb[head, rows - 1 : rows, :])
                    following = total * rbuf[step, j].astype(F32) + local[head]
                    sbuf[step, j] = following.astype(wire)
                state_copy(step).start()

        for j in range(pack):
            head = step * pack + j
            second[:, head_cols(head)] = finish(head, half, ibuf[j], rbuf[step, j].astype(BF16))

        @pl.when(jnp.logical_not(holds))
        def _():
            out_copy(step).start()

    @pl.when(holds)
    def _():
        @pl.loop(0, steps)
        def _(step):
            out_copy(step).start()

    @pl.loop(0, steps)
    def _(step):
        for j in range(pack):
            head = step * pack + j
            within = intra(head, 0, 0)
            first[:, head_cols(head)] = finish(head, 0, within, rbuf[step, j].astype(BF16))
        first_copy(step).start()

    @pl.loop(0, steps)
    def _(step):
        first_copy(step).wait()
        out_copy(step).wait_send()

        @pl.when(jnp.logical_not(is_last))
        def _():
            state_copy(step).wait_send()

    @pl.loop(0, steps)
    def _(step):
        out_copy(step).wait_recv()


def shards(count, queries, key_vectors, value_vectors, log_decay, out_gain):
    rows, features = queries.shape
    heads = log_decay.shape[1]
    width = features // heads
    pack = 2
    steps = heads // pack
    half = rows // 2
    wire = BF16 if count <= 8 else F32
    assert rows == BLOCK and count % 2 == 0 and heads % pack == 0
    anywhere = pl.BlockSpec(memory_space=pl.ANY)
    far = pl.BlockSpec(memory_space=pltpu.HBM)
    vmem = pl.BlockSpec(memory_space=pltpu.VMEM)
    return pl.pallas_call(
        functools.partial(kernel, count, heads, pack, wire),
        out_shape=jax.ShapeDtypeStruct((rows, features), BF16),
        in_specs=[far, far, far, vmem, vmem],
        out_specs=anywhere,
        scratch_shapes=[
            pltpu.VMEM((rows, features), BF16),
            pltpu.VMEM((rows, features), BF16),
            pltpu.VMEM((rows, features), BF16),
            pltpu.VMEM((heads, rows, width), F32),
            pltpu.VMEM((128, rows), F32),
            pltpu.VMEM((heads, width, width), F32),
            pltpu.VMEM((steps, pack, width, width), wire),
            pltpu.VMEM((steps, pack, width, width), wire),
            pltpu.VMEM((half, features), BF16),
            pltpu.VMEM((half, features), BF16),
            pltpu.VMEM((pack, half, width), F32),
            pltpu.SemaphoreType.DMA((3, steps)),
            pltpu.SemaphoreType.DMA((steps,)),
            pltpu.SemaphoreType.DMA((steps,)),
            pltpu.SemaphoreType.DMA((steps,)),
            pltpu.SemaphoreType.DMA((steps,)),
            pltpu.SemaphoreType.DMA((steps,)),
        ],
        compiler_params=pltpu.CompilerParams(
            collective_id=0, has_side_effects=True, vmem_limit_bytes=60 << 20
        ),
    )(queries, key_vectors, value_vectors, log_decay.T, out_gain.reshape(heads, width))


def solution(mesh):
    in_specs = (
        P(("group", "ctx"), "head"),
        P(("group", "ctx"), "head"),
        P(("group", "ctx"), "head"),
        P(("group", "ctx"), "head"),
        P("head"),
    )
    out_specs = P(("group", "ctx"), "head")
    return jax.shard_map(
        functools.partial(shards, mesh.shape["ctx"]),
        mesh=mesh,
        in_specs=in_specs,
        out_specs=out_specs,
        check_vma=False,
    )
```

```python
import functools

import jax
import jax.numpy as jnp
from jax import lax
from jax.experimental import pallas as pl
from jax.experimental.pallas import tpu as pltpu
from jax.sharding import PartitionSpec as P

BLOCK = 512
MESH = pl.DeviceIdType.MESH
F32 = jnp.float32
BF16 = jnp.bfloat16
CONTRACT_LAST = (((1,), (1,)), ((), ()))
CONTRACT_FIRST = (((0,), (0,)), ((), ()))


def kernel(
    count, heads, pack, wire,
    q_hbm, k_hbm, v_hbm, decay_ref, gain_ref, out_hbm,
    q, k, v, colb, rowc, local, rbuf, sbuf, first, second, ibuf,
    load_sem, state_send, state_recv, out_send, out_recv, first_sem, ready,
):
    rows, features = q.shape
    width = features // heads
    half = rows // 2
    steps = heads // pack
    span = pack * width
    me = lax.axis_index("ctx")
    mirror = count - 1 - me
    is_first = me == 0
    is_last = me == count - 1
    holds = jnp.logical_and(me > 0, me < mirror)

    def cols(step):
        return pl.ds(pl.multiple_of(step * span, span), span)

    def head_cols(head):
        return pl.ds(pl.multiple_of(head * width, width), width)

    def load(which, step):
        src, dst = ((k_hbm, k), (v_hbm, v), (q_hbm, q))[which]
        return pltpu.make_async_copy(
            src.at[:, cols(step)], dst.at[:, cols(step)], load_sem.at[which, step]
        )

    def state_copy(step):
        return pltpu.make_async_remote_copy(
            src_ref=sbuf.at[step],
            dst_ref=rbuf.at[step],
            send_sem=state_send.at[step],
            recv_sem=state_recv.at[step],
            device_id={"ctx": me + 1},
            device_id_type=MESH,
        )

    def out_copy(step):
        return pltpu.make_async_remote_copy(
            src_ref=second.at[:, cols(step)],
            dst_ref=out_hbm.at[pl.ds(half, half), cols(step)],
            send_sem=out_send.at[step],
            recv_sem=out_recv.at[step],
            device_id={"ctx": mirror},
            device_id_type=MESH,
        )

    def first_copy(step):
        return pltpu.make_async_copy(
            first.at[:, cols(step)], out_hbm.at[pl.ds(0, half), cols(step)], first_sem.at[step]
        )

    barrier = pltpu.get_barrier_semaphore()

    @pl.when(jnp.logical_not(is_first))
    def _():
        pl.semaphore_signal(barrier, inc=1, device_id={"ctx": me - 1}, device_id_type=MESH)

    @pl.when(jnp.logical_not(is_last))
    def _():
        pl.semaphore_signal(barrier, inc=1, device_id={"ctx": me + 1}, device_id_type=MESH)

    @pl.loop(0, steps)
    def _(step):
        load(0, step).start()
        load(1, step).start()

    @pl.loop(0, steps)
    def _(step):
        load(2, step).start()

    earlier = lax.broadcasted_iota(jnp.int32, (rows, rows), 0)
    later = lax.broadcasted_iota(jnp.int32, (rows, rows), 1)
    upto = jnp.where(earlier <= later, 1.0, 0.0).astype(BF16)
    rest = decay_ref[...]
    cum = jnp.zeros((heads, rows), F32)
    for _ in range(3):
        piece = rest.astype(BF16)
        rest = rest - piece.astype(F32)
        cum = cum + jnp.dot(piece, upto, preferred_element_type=F32)
    rowc[...] = jnp.zeros_like(rowc)
    rowc[0:heads, :] = cum
    columns = rowc[...].T
    for head in range(heads):
        colb[head] = jnp.broadcast_to(columns[:, head : head + 1], (rows, width))

    @pl.when(is_first)
    def _():
        rbuf[...] = jnp.zeros_like(rbuf)

    def forward(step):
        state_copy(step).wait_recv()

        @pl.when(jnp.logical_not(is_last))
        def _():
            for j in range(pack):
                head = step * pack + j
                total = jnp.exp(colb[head, rows - 1 : rows, :])
                following = total * rbuf[step, j].astype(F32) + local[head]
                sbuf[step, j] = following.astype(wire)
            state_copy(step).start()

    def states(step):
        load(0, step).wait()
        load(1, step).wait()
        for j in range(pack):
            head = step * pack + j
            here = head_cols(head)
            total = colb[head, rows - 1 : rows, :]
            decayed = (k[:, here].astype(F32) * jnp.exp(total - colb[head])).astype(BF16)
            state = lax.dot_general(decayed, v[:, here], CONTRACT_FIRST, preferred_element_type=F32)
            local[head] = state

            @pl.when(is_first)
            def _():
                sbuf[step, j] = state.astype(wire)

    def launch(step):
        @pl.when(is_first)
        def _():
            state_copy(step).start()

        @pl.when(holds)
        def _():
            forward(step)

    ahead = min(1, steps)
    pl.loop(0, ahead)(states)
    peers = (me + count - 1) // count + (mirror + count - 1) // count
    pl.semaphore_wait(barrier, peers)
    pl.loop(0, ahead)(launch)

    @pl.when(jnp.logical_and(jnp.logical_not(is_first), jnp.logical_not(is_last)))
    def _():
        pl.semaphore_wait(ready, 1)

    @pl.when(jnp.logical_not(is_first))
    def _():
        pl.semaphore_signal(ready, inc=1, device_id={"ctx": me - 1}, device_id_type=MESH)

    @pl.loop(ahead, steps)
    def _(step):
        states(step)
        launch(step)

    @pl.when(is_first)
    def _():
        pl.semaphore_wait(ready, 1)

    causal = lax.broadcasted_iota(jnp.int32, (half, half), 0) >= lax.broadcasted_iota(
        jnp.int32, (half, half), 1
    )

    def probs(head, low, start):
        queries = q[low : low + half, head_cols(head)]
        keys = k[start : start + half, head_cols(head)]
        scores = lax.dot_general(queries, keys, CONTRACT_LAST, preferred_element_type=F32)
        mine = colb[head, low : low + half, :]
        mine = jnp.concatenate([mine] * (half // width), axis=1)
        theirs = rowc[pl.ds(head, 1), start : start + half]
        weights = jnp.exp(jnp.minimum(mine - theirs, 0.0))
        if low == start:
            weights = jnp.where(causal, weights, 0.0)
        return (scores * weights).astype(BF16)

    def intra(head, low, start):
        return jnp.dot(
            probs(head, low, start),
            v[start : start + half, head_cols(head)],
            preferred_element_type=F32,
        )

    def finish(head, low, within, carried):
        queries = q[low : low + half, head_cols(head)].astype(F32)
        decayed = (queries * jnp.exp(colb[head, low : low + half, :])).astype(BF16)
        attn = within + jnp.dot(decayed, carried, preferred_element_type=F32)
        mean_square = jnp.mean(attn * attn, axis=-1, keepdims=True)
        normed = attn * lax.rsqrt(mean_square + 1e-06) * gain_ref[pl.ds(head, 1), :]
        return normed.astype(BF16)

    @pl.loop(0, steps)
    def _(step):
        load(2, step).wait()
        for j in range(pack):
            head = step * pack + j
            ibuf[j] = intra(head, half, 0) + intra(head, half, half)

        @pl.when(jnp.logical_not(jnp.logical_or(is_first, holds)))
        def _():
            forward(step)

        for j in range(pack):
            head = step * pack + j
            second[:, head_cols(head)] = finish(head, half, ibuf[j], rbuf[step, j].astype(BF16))

        out_copy(step).start()

    @pl.loop(0, steps)
    def _(step):
        for j in range(pack):
            head = step * pack + j
            within = intra(head, 0, 0)
            first[:, head_cols(head)] = finish(head, 0, within, rbuf[step, j].astype(BF16))
        first_copy(step).start()

    @pl.loop(0, steps)
    def _(step):
        first_copy(step).wait()
        out_copy(step).wait_send()

        @pl.when(jnp.logical_not(is_last))
        def _():
            state_copy(step).wait_send()

    @pl.loop(0, steps)
    def _(step):
        out_copy(step).wait_recv()


def shards(count, queries, key_vectors, value_vectors, log_decay, out_gain):
    rows, features = queries.shape
    heads = log_decay.shape[1]
    width = features // heads
    pack = 2
    steps = heads // pack
    half = rows // 2
    wire = BF16 if count <= 8 else F32
    assert rows == BLOCK and count % 2 == 0 and heads % pack == 0
    anywhere = pl.BlockSpec(memory_space=pl.ANY)
    far = pl.BlockSpec(memory_space=pltpu.HBM)
    vmem = pl.BlockSpec(memory_space=pltpu.VMEM)
    return pl.pallas_call(
        functools.partial(kernel, count, heads, pack, wire),
        out_shape=jax.ShapeDtypeStruct((rows, features), BF16),
        in_specs=[far, far, far, vmem, vmem],
        out_specs=anywhere,
        scratch_shapes=[
            pltpu.VMEM((rows, features), BF16),
            pltpu.VMEM((rows, features), BF16),
            pltpu.VMEM((rows, features), BF16),
            pltpu.VMEM((heads, rows, width), F32),
            pltpu.VMEM((128, rows), F32),
            pltpu.VMEM((heads, width, width), F32),
            pltpu.VMEM((steps, pack, width, width), wire),
            pltpu.VMEM((steps, pack, width, width), wire),
            pltpu.VMEM((half, features), BF16),
            pltpu.VMEM((half, features), BF16),
            pltpu.VMEM((pack, half, width), F32),
            pltpu.SemaphoreType.DMA((3, steps)),
            pltpu.SemaphoreType.DMA((steps,)),
            pltpu.SemaphoreType.DMA((steps,)),
            pltpu.SemaphoreType.DMA((steps,)),
            pltpu.SemaphoreType.DMA((steps,)),
            pltpu.SemaphoreType.DMA((steps,)),
            pltpu.SemaphoreType.REGULAR,
        ],
        compiler_params=pltpu.CompilerParams(
            collective_id=0, has_side_effects=True, vmem_limit_bytes=50 << 20
        ),
    )(queries, key_vectors, value_vectors, log_decay.T, out_gain.reshape(heads, width))


def solution(mesh):
    in_specs = (
        P(("group", "ctx"), "head"),
        P(("group", "ctx"), "head"),
        P(("group", "ctx"), "head"),
        P(("group", "ctx"), "head"),
        P("head"),
    )
    out_specs = P(("group", "ctx"), "head")
    return jax.shard_map(
        functools.partial(shards, mesh.shape["ctx"]),
        mesh=mesh,
        in_specs=in_specs,
        out_specs=out_specs,
        check_vma=False,
    )
```
